32 devices in a mesh: member: 2 (over y), row: 4 (over z), col: 2 (over x), sub: 2 (over core).
Axes of the slice: x: 2, y: 2, z: 4, core: 2. Of those that a mesh axis runs over, the one named last changes fastest.
Arguments:
- kernel: float32 [12288, 12288], P('row', ('col', 'sub')), may hold values from -0.0546875 to 0.0546875
- log_rate: float32 [512, 12288], P(('member', 'col', 'sub'), 'row'), parts along dimension 0, may hold values from -1 to 1
- state: float32 [512, 12288], P(('member', 'col', 'sub'), 'row'), parts along dimension 0, may hold values from -1 to 1
- base_stress: float32 [512, 12288], P(('member', 'col', 'sub'), 'row'), parts along dimension 0, may hold values from 1 to 4
- friction: float32 [12288], P('row'), may hold values from 0.5 to 2
- region: int32 [12288], P('row'), may hold values 0 or 1
- adjacency: int32 [12288], P('row'), may hold values from 0 to 12287, as said below
Outputs:
- final_rate: float32 [512, 12288], P(('member', 'col', 'sub'), 'row'), parts along dimension 0
- stress: float32 [512, 12288], P(('member', 'col', 'sub'), 'row'), parts along dimension 0
The draws below stay inside these ranges and needn't reach their ends.
There are 2 independent parts, one for each index of `member`. The reference program is written for one: setup_inputs(seed, part) draws one part's arguments, and reference() takes and returns one part's arrays. A program takes and returns all parts, laid end to end along the dimension named above; an argument that names none is the same for every part. Nothing has to cross between parts.
Inputs may be any that keep to these rules, and one draw needn't show every extreme that they name: `region`: 1 marks a volume cell, 0 a fault patch. `adjacency`: each unknown's partner lies in the same aligned block of 3072 unknowns.
All inputs are finite; a program needn't handle non-finite values. No bound on the sum of `region` on one device may be relied on, other than what follows from the above.
Results may differ from the reference program's by a relative error of at most 0.0003.
Values sent between devices are 32-bit elements; how exact they have to be, the bound alone decides.
A program may use at most 128 MiB of HBM per device.

```python
import math
import jax
import jax.numpy as jnp
from jax import lax

NU = 12288
SAMPLES = 256
NEWTON = 4
ROWB = 3072


def draw_adjacency(key, part):
    blocks = jnp.arange(NU, dtype=jnp.int32) // ROWB * ROWB
    offset = jax.random.randint(jax.random.fold_in(key, 17), (NU,), 0, ROWB, dtype=jnp.int32)
    return (blocks + offset).astype(jnp.int32)


def place_ends(drawn, stream_key, smallest, high):
    longest = drawn.shape.index(max(drawn.shape))
    spots = []
    for shift in (0, 1):
        where = [jax.random.randint(jax.random.fold_in(stream_key, axis), (), 0, length) for axis, length in enumerate(drawn.shape)]
        where[longest] = (where[longest] + shift) % drawn.shape[longest]
        spots.append(tuple(where))
    return drawn.at[spots[0]].set(smallest).at[spots[1]].set(high)


def level_of(stream_key, shape, cuts, least, high):
    def one(position, blocks):
        heights = jax.random.uniform(jax.random.fold_in(jax.random.fold_in(stream_key, 6), position), (blocks,), jnp.float32, least / len(cuts), high / len(cuts))
        return jnp.repeat(jnp.exp(heights), shape[position] // blocks).reshape((-1,) + (1,) * (len(shape) - position - 1))

    loudness = one(*cuts[0])
    for cut in cuts[1:]:
        loudness = loudness * one(*cut)
    return loudness


def scatter_about(stream_key, extent, deviation, limit, split=(), kind=jnp.bfloat16):
    result = deviation * jax.random.normal(stream_key, extent, jnp.float32)
    if split:
        result = result * level_of(stream_key, extent, split, -0.22, 0.18)
    return jnp.clip(result, -limit, limit).astype(kind)


def setup_inputs(seed: int = 0, part: int = 0) -> dict:
    keys = jax.random.split(jax.random.key(seed), 8)
    part_splits = jax.random.split(jax.random.fold_in(keys[7], part), 8)
    kernel = scatter_about(keys[0], (NU, NU), NU ** -0.5, 0.0546875, ((0, 4), (1, 4)), jnp.float32)
    log_rate = jnp.clip(jax.random.uniform(part_splits[1], (SAMPLES, NU), jnp.float32, -1.0, 1.0) * level_of(part_splits[1], (SAMPLES, NU), ((0, 4), (1, 4)), -0.4, 0.0), -1.0, 1.0)
    state = jnp.clip(jax.random.uniform(part_splits[2], (SAMPLES, NU), jnp.float32, -1.0, 1.0) * level_of(part_splits[2], (SAMPLES, NU), ((0, 4), (1, 4)), -0.4, 0.0), -1.0, 1.0)
    base_stress = jnp.clip(1.0 + 3.0 * jax.random.uniform(part_splits[3], (SAMPLES, NU), jnp.float32) ** level_of(part_splits[3], (SAMPLES, NU), ((0, 4), (1, 4)), -0.2, 0.2), 1.0, 4.0)
    friction = jnp.clip(jnp.exp(math.log(2.0) - 1.3862944 * jax.random.uniform(keys[4], (NU,), jnp.float32) ** level_of(keys[4], (NU,), ((0, 4),), -0.2, 0.2)), 0.5, 2.0)
    region = place_ends((jax.random.randint(keys[5], (NU,), 0, 3) < 1).astype(jnp.int32), jax.random.fold_in(keys[5], 1), 0, 1)
    adjacency = draw_adjacency(jax.random.fold_in(keys[7], 71), part)
    return dict(kernel=kernel, log_rate=log_rate, state=state, base_stress=base_stress, friction=friction, region=region, adjacency=adjacency)


coupling = 0.3
step_size = 0.5

def couple(stress, adjacency):
    return stress + coupling * (jnp.take(stress, adjacency, axis=1) - stress)

def solve(log_rate, state, stress, friction, volume):
    value = log_rate
    for turn in range(NEWTON):
        expo = jnp.exp(value)
        slipx = jnp.exp(value + state)
        root = jnp.sqrt(1.0 + slipx * slipx)
        fault_f = friction * jnp.log(slipx + root)
        fault_d = friction * slipx / root
        creep = jnp.exp(state + value / 3.0)
        cell_f = friction * creep
        cell_d = friction * creep / 3.0
        resid = jnp.where(volume, cell_f, fault_f) + expo - stress
        deriv = jnp.where(volume, cell_d, fault_d) + expo
        value = value - jnp.clip(resid / deriv, -1.0, 1.0)
    return value

def rates_times(rates, kernel):
    return lax.dot_general(rates, kernel, (((1,), (1,)), ((), ())), precision=lax.Precision.HIGHEST, preferred_element_type=jnp.float32)

def reference(kernel, log_rate, state, base_stress, friction, region, adjacency):
    volume = (region == 1)[None, :]
    fric = friction[None, :]
    first = rates_times(jnp.exp(log_rate), kernel)
    section_one = solve(log_rate, state, couple(base_stress + step_size * first, adjacency), fric, volume)
    second = rates_times(jnp.exp(section_one), kernel)
    stress = couple(base_stress + 0.5 * step_size * (first + second), adjacency)
    final_rate = solve(section_one, state, stress, fric, volume)
    return (final_rate, stress)
```

```python
import jax
import jax.numpy as jnp
from jax import lax
from jax.sharding import PartitionSpec as P

NEWTON = 4


coupling = 0.3
step_size = 0.5


def couple(stress, partner):
    return stress + coupling * (jnp.take(stress, partner, axis=1) - stress)


def solve(log_rate, state, stress, friction, volume):
    value = log_rate
    for turn in range(NEWTON):
        expo = jnp.exp(value)
        slipx = jnp.exp(value + state)
        root = jnp.sqrt(1.0 + slipx * slipx)
        fault_f = friction * jnp.log(slipx + root)
        fault_d = friction * slipx / root
        creep = jnp.exp(state + value / 3.0)
        cell_f = friction * creep
        cell_d = friction * creep / 3.0
        resid = jnp.where(volume, cell_f, fault_f) + expo - stress
        deriv = jnp.where(volume, cell_d, fault_d) + expo
        value = value - jnp.clip(resid / deriv, -1.0, 1.0)
    return value


def rates_times(rates, kernel):
    return lax.dot_general(
        rates,
        kernel,
        (((1,), (1,)), ((), ())),
        precision=lax.Precision.HIGH,
        preferred_element_type=jnp.float32,
    )


def per_device(kernel, log_rate, state, base_stress, friction, region, adjacency):
    rows = kernel.shape[0]
    partner = adjacency - lax.axis_index("row") * rows
    volume = (region == 1)[None, :]
    fric = friction[None, :]

    def spread(rates):
        whole = lax.all_gather(rates, "row", axis=1, tiled=True)
        return lax.all_to_all(
            whole, ("col", "sub"), split_axis=1, concat_axis=0, tiled=True
        )

    def total(columns):
        return lax.psum_scatter(
            rates_times(columns, kernel), ("col", "sub"), scatter_dimension=0, tiled=True
        )

    first = total(spread(jnp.exp(log_rate)))
    section_one = solve(
        log_rate, state, couple(base_stress + step_size * first, partner), fric, volume
    )
    second = total(spread(jnp.exp(section_one)))
    stress = couple(base_stress + 0.5 * step_size * (first + second), partner)
    final_rate = solve(section_one, state, stress, fric, volume)
    return (final_rate, stress)


def solution(mesh):
    in_specs = (
        P("row", ("col", "sub")),
        P(("member", "col", "sub"), "row"),
        P(("member", "col", "sub"), "row"),
        P(("member", "col", "sub"), "row"),
        P("row"),
        P("row"),
        P("row"),
    )
    out_specs = (P(("member", "col", "sub"), "row"), P(("member", "col", "sub"), "row"))
    return jax.shard_map(
        per_device, mesh=mesh, in_specs=in_specs, out_specs=out_specs, check_vma=False
    )
```

```python
import functools

import jax
import jax.numpy as jnp
from jax import lax
from jax.experimental import pallas as pl
from jax.experimental.pallas import tpu as pltpu
from jax.sharding import PartitionSpec as P

NEWTON = 4


coupling = 0.3
step_size = 0.5

MESH = pl.DeviceIdType.MESH


def couple(stress, partner):
    return stress + coupling * (jnp.take(stress, partner, axis=1) - stress)


def solve(log_rate, state, stress, friction, volume):
    value = log_rate
    for turn in range(NEWTON):
        expo = jnp.exp(value)
        slipx = jnp.exp(value + state)
        root = jnp.sqrt(1.0 + slipx * slipx)
        fault_f = friction * jnp.log(slipx + root)
        fault_d = friction * slipx / root
        creep = jnp.exp(state + value / 3.0)
        cell_f = friction * creep
        cell_d = friction * creep / 3.0
        resid = jnp.where(volume, cell_f, fault_f) + expo - stress
        deriv = jnp.where(volume, cell_d, fault_d) + expo
        value = value - jnp.clip(resid / deriv, -1.0, 1.0)
    return value


def split(value):
    high = value.astype(jnp.bfloat16)
    return high, (value - high.astype(jnp.float32)).astype(jnp.bfloat16)


def times(left, right):
    return lax.dot_general(
        left, right, (((1,), (1,)), ((), ())), preferred_element_type=jnp.float32
    )


def step_kernel(
    R, C, S, Q,
    x_ref, k_ref, out_ref,
    held, wide, kern, xhigh, xlow, acc, pair_in, col_in,
    x_sem, k_sem, held_recv, up_send, down_send,
    wide_recv, wide_send, pair_recv, pair_send, col_recv, col_send,
):
    r = lax.axis_index("row")
    c = lax.axis_index("col")
    s = lax.axis_index("sub")
    j = c * S + s
    slot = s * C + c
    B, D = x_ref.shape
    CW = D // Q

    def cols(q):
        return pl.ds(pl.multiple_of(q * CW, CW), CW)

    def x_copy(q):
        return pltpu.make_async_copy(x_ref.at[:, cols(q)], held.at[q, r], x_sem.at[q])

    def k_copy(q):
        return pltpu.make_async_copy(k_ref.at[:, cols(q)], kern.at[q], k_sem.at[q])

    def chain(q, b, sends, row):
        return pltpu.make_async_remote_copy(
            src_ref=held.at[q, b], dst_ref=held.at[q, b],
            send_sem=sends.at[q, b], recv_sem=held_recv.at[q, b],
            device_id={"row": row}, device_id_type=MESH,
        )

    def up(q, b):
        return chain(q, b, up_send, r + 1)

    def down(q, b):
        return chain(q, b, down_send, r - 1)

    def plane(q, b, where):
        return pltpu.make_async_remote_copy(
            src_ref=held.at[q, b], dst_ref=wide.at[q, where],
            send_sem=wide_send.at[q, b], recv_sem=wide_recv.at[q, where],
            device_id={"col": b // S, "sub": b % S}, device_id_type=MESH,
        )

    def pair(p):
        return pltpu.make_async_remote_copy(
            src_ref=acc.at[p, 1 - s], dst_ref=pair_in.at[p],
            send_sem=pair_send.at[p], recv_sem=pair_recv.at[p],
            device_id={"sub": 1 - s}, device_id_type=MESH,
        )

    def across(p, to, where):
        return pltpu.make_async_remote_copy(
            src_ref=acc.at[p, s, to], dst_ref=col_in.at[p, where],
            send_sem=col_send.at[p, to], recv_sem=col_recv.at[p, where],
            device_id={"col": to}, device_id_type=MESH,
        )

    def pass_plane(q, b):
        @pl.when(b != j)
        def _():
            plane(q, b, slot).start()

    def start_own(q):
        x_copy(q).wait()

        @pl.when(r < R - 1)
        def _():
            up(q, r).start()

        @pl.when(r > 0)
        def _():
            down(q, r).start()

        pass_plane(q, r)

    for q in range(Q):
        x_copy(q).start()
    for q in range(Q):
        k_copy(q).start()

    barrier = pltpu.get_barrier_semaphore()

    @pl.when(r < R - 1)
    def _():
        pl.semaphore_signal(barrier, inc=1, device_id={"row": r + 1}, device_id_type=MESH)

    @pl.when(r > 0)
    def _():
        pl.semaphore_signal(barrier, inc=1, device_id={"row": r - 1}, device_id_type=MESH)

    for other in range(C * S):
        @pl.when(other != j)
        def _():
            pl.semaphore_signal(
                barrier, inc=1,
                device_id={"col": other // S, "sub": other % S}, device_id_type=MESH,
            )

    ends = (r > 0).astype(jnp.int32) + (r < R - 1).astype(jnp.int32)
    pl.semaphore_wait(barrier, C * S - 1 + ends)

    def pass_on(q, t):
        below = r - t
        above = r + t

        @pl.when(below >= 0)
        def _():
            up(q, below).wait_recv()

            @pl.when(r < R - 1)
            def _():
                up(q, below).start()

            pass_plane(q, below)

        @pl.when(above < R)
        def _():
            down(q, above).wait_recv()

            @pl.when(r > 0)
            def _():
                down(q, above).start()

            pass_plane(q, above)

    def load_sources(q):
        for g in range(C * S):
            at = pl.ds(g * B, B)

            def put(value):
                high, low = split(value)
                xhigh[at, :] = high
                xlow[at, :] = low

            @pl.when(g != slot)
            def _():
                plane(q, j, g).wait_recv()
                put(wide[q, g])

            @pl.when(g == slot)
            def _():
                put(held[q, j])

    def tile(q, p):
        khigh, klow = split(kern[q, cols(p), :])
        high = xhigh[...]
        part = times(high, khigh) + (times(high, klow) + times(xlow[...], khigh))
        part = part.reshape(S, C, B, CW)
        acc[p] = acc[p] + part

    start_own(0)
    if Q > 1:
        start_own(1)

    def clear(p, carry):
        acc[p] = jnp.zeros_like(acc[p])
        return carry

    lax.fori_loop(0, Q, clear, 0)
    cuts = [(Q * t) // (R - 1) for t in range(R)]

    def chunk(q, carry):
        for t in range(1, R):
            pass_on(q, t)
            if t == 1:
                @pl.when(q + 2 < Q)
                def _():
                    start_own(q + 2)

                @pl.when(q > 0)
                def _():
                    load_sources(q - 1)
                    k_copy(q - 1).wait()

            if cuts[t] > cuts[t - 1]:
                @pl.when(q > 0)
                def _():
                    def run(p, inner):
                        tile(q - 1, p)
                        return inner

                    lax.fori_loop(cuts[t - 1], cuts[t], run, 0)
        return carry

    lax.fori_loop(0, Q, chunk, 0)
    load_sources(Q - 1)
    k_copy(Q - 1).wait()

    def add_pair(p):
        pair(p).wait_recv()
        acc[p, s] = acc[p, s] + pair_in[p]
        for to in range(C):
            @pl.when(to != c)
            def _():
                across(p, to, c).start()

    def last(p, carry):
        tile(Q - 1, p)
        pair(p).start()

        @pl.when(p > 0)
        def _():
            add_pair(p - 1)

        return carry

    lax.fori_loop(0, Q, last, 0)
    add_pair(Q - 1)

    def finish(p, carry):
        out_ref[:, cols(p)] = acc[p, s, c]
        for other in range(C):
            @pl.when(other != c)
            def _():
                across(p, c, other).wait_recv()
                out_ref[:, cols(p)] = out_ref[:, cols(p)] + col_in[p, other]
        return carry

    lax.fori_loop(0, Q, finish, 0)

    def drain(q, carry):
        pair(q).wait_send()
        for to in range(C):
            @pl.when(to != c)
            def _():
                across(q, to, c).wait_send()
        for b in range(R):
            @pl.when((b <= r) & (r < R - 1))
            def _():
                up(q, b).wait_send()

            @pl.when((b >= r) & (r > 0))
            def _():
                down(q, b).wait_send()

            @pl.when(b != j)
            def _():
                plane(q, b, slot).wait_send()
        return carry

    lax.fori_loop(0, Q, drain, 0)


def chunks_of(D):
    lanes = D // 128
    for count in (6, 5, 4, 3, 2):
        if D % 128 == 0 and lanes % count == 0:
            return count
    return 1


def step_call(R, C, S, rates, kernel):
    B, D = rates.shape
    Q = chunks_of(D)
    CW = D // Q
    dma = pltpu.SemaphoreType.DMA
    f32, b16 = jnp.float32, jnp.bfloat16
    return pl.pallas_call(
        functools.partial(step_kernel, R, C, S, Q),
        out_shape=jax.ShapeDtypeStruct((B, D), f32),
        in_specs=[pl.BlockSpec(memory_space=pl.ANY)] * 2,
        out_specs=pl.BlockSpec(memory_space=pltpu.VMEM),
        scratch_shapes=[
            pltpu.VMEM((Q, R, B, CW), f32),
            pltpu.VMEM((Q, C * S, B, CW), f32),
            pltpu.VMEM((Q, D, CW), f32),
            pltpu.VMEM((C * S * B, CW), b16),
            pltpu.VMEM((C * S * B, CW), b16),
            pltpu.VMEM((Q, S, C, B, CW), f32),
            pltpu.VMEM((Q, C, B, CW), f32),
            pltpu.VMEM((Q, C, B, CW), f32),
            dma((Q,)),
            dma((Q,)),
            dma((Q, R)),
            dma((Q, R)),
            dma((Q, R)),
            dma((Q, C * S)),
            dma((Q, R)),
            dma((Q,)),
            dma((Q,)),
            dma((Q, C)),
            dma((Q, C)),
        ],
        compiler_params=pltpu.CompilerParams(
            collective_id=0, has_side_effects=True, vmem_limit_bytes=62 * 1024 * 1024
        ),
    )(rates, kernel)


def per_device(R, C, S, kernel, log_rate, state, base_stress, friction, region, adjacency):
    rows = kernel.shape[0]
    partner = adjacency - lax.axis_index("row") * rows
    volume = (region == 1)[None, :]
    fric = friction[None, :]

    first = step_call(R, C, S, jnp.exp(log_rate), kernel)
    section_one = solve(
        log_rate, state, couple(base_stress + step_size * first, partner), fric, volume
    )
    second = step_call(R, C, S, jnp.exp(section_one), kernel)
    stress = couple(base_stress + 0.5 * step_size * (first + second), partner)
    final_rate = solve(section_one, state, stress, fric, volume)
    return (final_rate, stress)


def solution(mesh):
    R, C, S = mesh.shape["row"], mesh.shape["col"], mesh.shape["sub"]
    assert R == C * S and S == 2
    in_specs = (
        P("row", ("col", "sub")),
        P(("member", "col", "sub"), "row"),
        P(("member", "col", "sub"), "row"),
        P(("member", "col", "sub"), "row"),
        P("row"),
        P("row"),
        P("row"),
    )
    out_specs = (P(("member", "col", "sub"), "row"), P(("member", "col", "sub"), "row"))
    return jax.shard_map(
        functools.partial(per_device, R, C, S),
        mesh=mesh, in_specs=in_specs, out_specs=out_specs, check_vma=False,
    )
```

```python
import functools

import jax
import jax.numpy as jnp
from jax import lax
from jax.experimental import pallas as pl
from jax.experimental.pallas import tpu as pltpu
from jax.sharding import PartitionSpec as P

NEWTON = 4


coupling = 0.3
step_size = 0.5

MESH = pl.DeviceIdType.MESH


def couple(stress, partner):
    return stress + coupling * (jnp.take(stress, partner, axis=1) - stress)


def solve(log_rate, state, stress, friction, volume):
    value = log_rate
    for turn in range(NEWTON):
        expo = jnp.exp(value)
        slipx = jnp.exp(value + state)
        root = jnp.sqrt(1.0 + slipx * slipx)
        fault_f = friction * jnp.log(slipx + root)
        fault_d = friction * slipx / root
        creep = jnp.exp(state + value / 3.0)
        cell_f = friction * creep
        cell_d = friction * creep / 3.0
        resid = jnp.where(volume, cell_f, fault_f) + expo - stress
        deriv = jnp.where(volume, cell_d, fault_d) + expo
        value = value - jnp.clip(resid / deriv, -1.0, 1.0)
    return value


def split(value):
    high = value.astype(jnp.bfloat16)
    return high, (value - high.astype(jnp.float32)).astype(jnp.bfloat16)


def times(left, right):
    return lax.dot_general(
        left, right, (((1,), (1,)), ((), ())), preferred_element_type=jnp.float32
    )


def step_kernel(
    R, C, S, H, Q, N,
    x_ref, k_ref, out_ref,
    held, wide, kern, xhigh, xlow, acc, pair_in, col_in,
    x_sem, k_sem, held_recv, up_send, down_send,
    wide_recv, wide_send, pair_recv, pair_send, col_recv, col_send,
):
    r = lax.axis_index("row")
    c = lax.axis_index("col")
    s = lax.axis_index("sub")
    j = c * S + s
    slot = s * C + c
    D = x_ref.shape[1]
    B = x_ref.shape[0] // H
    CW, NW = D // Q, D // N
    T = H * Q

    def cols(q):
        return pl.ds(pl.multiple_of(q * CW, CW), CW)

    def targets(p):
        return pl.ds(pl.multiple_of(p * NW, NW), NW)

    def part_of(q):
        return pl.ds(pl.multiple_of((q // Q) * B, B), B)

    def x_copy(q):
        return pltpu.make_async_copy(
            x_ref.at[part_of(q), cols(q % Q)], held.at[q, r], x_sem.at[q]
        )

    def k_copy(q):
        return pltpu.make_async_copy(k_ref.at[:, cols(q)], kern.at[q], k_sem.at[q])

    def chain(q, b, sends, row):
        return pltpu.make_async_remote_copy(
            src_ref=held.at[q, b], dst_ref=held.at[q, b],
            send_sem=sends.at[q, b], recv_sem=held_recv.at[q, b],
            device_id={"row": row}, device_id_type=MESH,
        )

    def up(q, b):
        return chain(q, b, up_send, r + 1)

    def down(q, b):
        return chain(q, b, down_send, r - 1)

    def plane(q, b, where):
        return pltpu.make_async_remote_copy(
            src_ref=held.at[q, b], dst_ref=wide.at[q, where],
            send_sem=wide_send.at[q, b], recv_sem=wide_recv.at[q, where],
            device_id={"col": b // S, "sub": b % S}, device_id_type=MESH,
        )

    def pair(p):
        return pltpu.make_async_remote_copy(
            src_ref=acc.at[p, 1 - s], dst_ref=pair_in.at[p],
            send_sem=pair_send.at[p], recv_sem=pair_recv.at[p],
            device_id={"sub": 1 - s}, device_id_type=MESH,
        )

    def across(p, to, where):
        return pltpu.make_async_remote_copy(
            src_ref=acc.at[p, s, to], dst_ref=col_in.at[p, where],
            send_sem=col_send.at[p, to], recv_sem=col_recv.at[p, where],
            device_id={"col": to}, device_id_type=MESH,
        )

    def pass_plane(q, b):
        @pl.when(b != j)
        def _():
            plane(q, b, slot).start()

    def start_own(q):
        x_copy(q).wait()

        @pl.when(r < R - 1)
        def _():
            up(q, r).start()

        @pl.when(r > 0)
        def _():
            down(q, r).start()

        pass_plane(q, r)

    for q in range(T):
        x_copy(q).start()
    for q in range(Q):
        k_copy(q).start()

    barrier = pltpu.get_barrier_semaphore()

    @pl.when(r < R - 1)
    def _():
        pl.semaphore_signal(barrier, inc=1, device_id={"row": r + 1}, device_id_type=MESH)

    @pl.when(r > 0)
    def _():
        pl.semaphore_signal(barrier, inc=1, device_id={"row": r - 1}, device_id_type=MESH)

    for other in range(C * S):
        @pl.when(other != j)
        def _():
            pl.semaphore_signal(
                barrier, inc=1,
                device_id={"col": other // S, "sub": other % S}, device_id_type=MESH,
            )

    ends = (r > 0).astype(jnp.int32) + (r < R - 1).astype(jnp.int32)
    pl.semaphore_wait(barrier, C * S - 1 + ends)

    def pass_on(q, t):
        below = r - t
        above = r + t

        @pl.when(below >= 0)
        def _():
            up(q, below).wait_recv()

            @pl.when(r < R - 1)
            def _():
                up(q, below).start()

            pass_plane(q, below)

        @pl.when(above < R)
        def _():
            down(q, above).wait_recv()

            @pl.when(r > 0)
            def _():
                down(q, above).start()

            pass_plane(q, above)

    def load_sources(q):
        for g in range(C * S):
            at = pl.ds(g * B, B)

            def put(value):
                high, low = split(value)
                xhigh[at, :] = high
                xlow[at, :] = low

            @pl.when(g != slot)
            def _():
                plane(q, j, g).wait_recv()
                put(wide[q, g])

            @pl.when(g == slot)
            def _():
                put(held[q, j])

    def tile(q, p):
        khigh, klow = split(kern[q % Q, targets(p), :])
        high = xhigh[...]
        part = times(high, khigh) + (times(high, klow) + times(xlow[...], khigh))
        at = (q // Q) * N + p
        acc[at] = acc[at] + part.reshape(S, C, B, NW)

    def add_pair(p):
        pair(p).wait_recv()
        acc[p, s] = acc[p, s] + pair_in[p]
        for to in range(C):
            @pl.when(to != c)
            def _():
                across(p, to, c).start()

    start_own(0)
    if T > 1:
        start_own(1)

    def clear(p, carry):
        acc[p] = jnp.zeros_like(acc[p])
        return carry

    lax.fori_loop(0, H * N, clear, 0)
    cuts = [(N * t) // (R - 1) for t in range(R)]

    def chunk(q, carry):
        done = (q - 1) // Q

        for t in range(1, R):
            pass_on(q, t)
            if t == 1:
                @pl.when(q + 2 < T)
                def _():
                    start_own(q + 2)

                @pl.when(q > 0)
                def _():
                    load_sources(q - 1)

                @pl.when((q > 0) & (q <= Q))
                def _():
                    k_copy(q - 1).wait()

            if cuts[t] > cuts[t - 1]:
                @pl.when(q > 0)
                def _():
                    def run(p, inner):
                        tile(q - 1, p)

                        @pl.when(q % Q == 0)
                        def _():
                            pair(done * N + p).start()

                        return inner

                    lax.fori_loop(cuts[t - 1], cuts[t], run, 0)

                @pl.when((q > Q) & (q % Q == 1 % Q))
                def _():
                    def run(p, inner):
                        add_pair((done - 1) * N + p)
                        return inner

                    lax.fori_loop(cuts[t - 1], cuts[t], run, 0)
        return carry

    lax.fori_loop(0, T, chunk, 0)
    load_sources(T - 1)
    if H == 1:
        k_copy(Q - 1).wait()

    def last(p, carry):
        tile(T - 1, p)
        pair((H - 1) * N + p).start()

        @pl.when(p > 0)
        def _():
            add_pair((H - 1) * N + p - 1)

        return carry

    lax.fori_loop(0, N, last, 0)
    add_pair(H * N - 1)

    def finish(p, carry):
        at = (part_of((p // N) * Q), targets(p % N))
        total = acc[p, s, c]
        out_ref[at] = total
        for other in range(C):
            @pl.when(other != c)
            def _():
                across(p, c, other).wait_recv()
                out_ref[at] = out_ref[at] + col_in[p, other]
        return carry

    lax.fori_loop(0, H * N, finish, 0)

    def drain_sums(p, carry):
        pair(p).wait_send()
        for to in range(C):
            @pl.when(to != c)
            def _():
                across(p, to, c).wait_send()
        return carry

    lax.fori_loop(0, H * N, drain_sums, 0)

    def drain(q, carry):
        for b in range(R):
            @pl.when((b <= r) & (r < R - 1))
            def _():
                up(q, b).wait_send()

            @pl.when((b >= r) & (r > 0))
            def _():
                down(q, b).wait_send()

            @pl.when(b != j)
            def _():
                plane(q, b, slot).wait_send()
        return carry

    lax.fori_loop(0, T, drain, 0)


def cut_of(D, most):
    lanes = D // 128
    for count in range(most, 1, -1):
        if D % 128 == 0 and lanes % count == 0:
            return count
    return 1


def step_call(R, C, S, rates, kernel):
    B, D = rates.shape
    H = 2 if B % 32 == 0 else 1
    B = B // H
    Q, N = cut_of(D, 3), cut_of(D, 6)
    assert Q > 1
    T, CW, NW = H * Q, D // Q, D // N
    dma = pltpu.SemaphoreType.DMA
    f32, b16 = jnp.float32, jnp.bfloat16
    return pl.pallas_call(
        functools.partial(step_kernel, R, C, S, H, Q, N),
        out_shape=jax.ShapeDtypeStruct(rates.shape, f32),
        in_specs=[pl.BlockSpec(memory_space=pl.ANY)] * 2,
        out_specs=pl.BlockSpec(memory_space=pltpu.VMEM),
        scratch_shapes=[
            pltpu.VMEM((T, R, B, CW), f32),
            pltpu.VMEM((T, C * S, B, CW), f32),
            pltpu.VMEM((Q, D, CW), f32),
            pltpu.VMEM((C * S * B, CW), b16),
            pltpu.VMEM((C * S * B, CW), b16),
            pltpu.VMEM((H * N, S, C, B, NW), f32),
            pltpu.VMEM((H * N, C, B, NW), f32),
            pltpu.VMEM((H * N, C, B, NW), f32),
            dma((T,)),
            dma((Q,)),
            dma((T, R)),
            dma((T, R)),
            dma((T, R)),
            dma((T, C * S)),
            dma((T, R)),
            dma((H * N,)),
            dma((H * N,)),
            dma((H * N, C)),
            dma((H * N, C)),
        ],
        compiler_params=pltpu.CompilerParams(
            collective_id=0, has_side_effects=True, vmem_limit_bytes=62 * 1024 * 1024
        ),
    )(rates, kernel)


def per_device(R, C, S, kernel, log_rate, state, base_stress, friction, region, adjacency):
    rows = kernel.shape[0]
    partner = adjacency - lax.axis_index("row") * rows
    volume = (region == 1)[None, :]
    fric = friction[None, :]

    first = step_call(R, C, S, jnp.exp(log_rate), kernel)
    section_one = solve(
        log_rate, state, couple(base_stress + step_size * first, partner), fric, volume
    )
    second = step_call(R, C, S, jnp.exp(section_one), kernel)
    stress = couple(base_stress + 0.5 * step_size * (first + second), partner)
    final_rate = solve(section_one, state, stress, fric, volume)
    return (final_rate, stress)


def solution(mesh):
    R, C, S = mesh.shape["row"], mesh.shape["col"], mesh.shape["sub"]
    assert R == C * S and S == 2
    in_specs = (
        P("row", ("col", "sub")),
        P(("member", "col", "sub"), "row"),
        P(("member", "col", "sub"), "row"),
        P(("member", "col", "sub"), "row"),
        P("row"),
        P("row"),
        P("row"),
    )
    out_specs = (P(("member", "col", "sub"), "row"), P(("member", "col", "sub"), "row"))
    return jax.shard_map(
        functools.partial(per_device, R, C, S),
        mesh=mesh, in_specs=in_specs, out_specs=out_specs, check_vma=False,
    )
```

```python
import functools

import jax
import jax.numpy as jnp
from jax import lax
from jax.experimental import pallas as pl
from jax.experimental.pallas import tpu as pltpu
from jax.sharding import PartitionSpec as P

NEWTON = 4


coupling = 0.3
step_size = 0.5

MESH = pl.DeviceIdType.MESH


def couple_kernel(parts, factor, base_ref, *refs):
    added, partner_ref, out_ref, whole = refs[:parts], refs[parts], refs[-2], refs[-1]
    B, D = base_ref.shape
    total = added[0][...]
    for ref in added[1:]:
        total = total + ref[...]
    whole[...] = base_ref[...] + factor * total

    def lanes(block, carry):
        at = pl.ds(pl.multiple_of(block * 128, 128), 128)
        index = jnp.broadcast_to(partner_ref[:, at], (B, 128))
        lane, source = index % 128, index // 128
        there = jnp.zeros((B, 128), jnp.float32)
        for k in range(D // 128):
            piece = jnp.take_along_axis(
                whole[:, k * 128 : (k + 1) * 128], lane, axis=1, mode="promise_in_bounds"
            )
            there = jnp.where(source == k, piece, there)
        here = whole[:, at]
        out_ref[:, at] = here + coupling * (there - here)
        return carry

    lax.fori_loop(0, D // 128, lanes, 0)


def coupled(base, factor, added, partner):
    return pl.pallas_call(
        functools.partial(couple_kernel, len(added), factor),
        out_shape=jax.ShapeDtypeStruct(base.shape, jnp.float32),
        in_specs=[pl.BlockSpec(memory_space=pltpu.VMEM)] * (len(added) + 2),
        out_specs=pl.BlockSpec(memory_space=pltpu.VMEM),
        scratch_shapes=[pltpu.VMEM(base.shape, jnp.float32)],
    )(base, *added, partner[None, :])


def solve(log_rate, state, stress, friction, volume):
    value = log_rate
    for turn in range(NEWTON):
        expo = jnp.exp(value)
        slipx = jnp.exp(value + state)
        root = jnp.sqrt(1.0 + slipx * slipx)
        fault_f = friction * jnp.log(slipx + root)
        fault_d = friction * slipx / root
        creep = jnp.exp(state + value / 3.0)
        cell_f = friction * creep
        cell_d = friction * creep / 3.0
        resid = jnp.where(volume, cell_f, fault_f) + expo - stress
        deriv = jnp.where(volume, cell_d, fault_d) + expo
        value = value - jnp.clip(resid / deriv, -1.0, 1.0)
    return value


def split(value):
    high = value.astype(jnp.bfloat16)
    return high, (value - high.astype(jnp.float32)).astype(jnp.bfloat16)


def times(left, right):
    return lax.dot_general(
        left, right, (((1,), (1,)), ((), ())), preferred_element_type=jnp.float32
    )


def step_kernel(
    R, C, S, H, Q, N,
    x_ref, k_ref, out_ref,
    held, wide, kern, xhigh, xlow, acc, pair_in, col_in,
    x_sem, k_sem, held_recv, up_send, down_send,
    wide_recv, wide_send, pair_recv, pair_send, col_recv, col_send,
):
    r = lax.axis_index("row")
    c = lax.axis_index("col")
    s = lax.axis_index("sub")
    j = c * S + s
    slot = s * C + c
    D = x_ref.shape[1]
    B = x_ref.shape[0] // H
    CW, NW = D // Q, D // N
    T = H * Q

    def cols(q):
        return pl.ds(pl.multiple_of(q * CW, CW), CW)

    def targets(p):
        return pl.ds(pl.multiple_of(p * NW, NW), NW)

    def part_of(q):
        return pl.ds(pl.multiple_of((q // Q) * B, B), B)

    def x_copy(q):
        return pltpu.make_async_copy(
            x_ref.at[part_of(q), cols(q % Q)], held.at[q, r], x_sem.at[q]
        )

    def k_copy(q):
        return pltpu.make_async_copy(k_ref.at[:, cols(q)], kern.at[q], k_sem.at[q])

    def chain(q, b, sends, row):
        return pltpu.make_async_remote_copy(
            src_ref=held.at[q, b], dst_ref=held.at[q, b],
            send_sem=sends.at[q, b], recv_sem=held_recv.at[q, b],
            device_id={"row": row}, device_id_type=MESH,
        )

    def up(q, b):
        return chain(q, b, up_send, r + 1)

    def down(q, b):
        return chain(q, b, down_send, r - 1)

    def plane(q, b, where):
        return pltpu.make_async_remote_copy(
            src_ref=held.at[q, b], dst_ref=wide.at[q, where],
            send_sem=wide_send.at[q, b], recv_sem=wide_recv.at[q, where],
            device_id={"col": b // S, "sub": b % S}, device_id_type=MESH,
        )

    def pair(p):
        return pltpu.make_async_remote_copy(
            src_ref=acc.at[p, 1 - s], dst_ref=pair_in.at[p],
            send_sem=pair_send.at[p], recv_sem=pair_recv.at[p],
            device_id={"sub": 1 - s}, device_id_type=MESH,
        )

    def across(p, to, where):
        return pltpu.make_async_remote_copy(
            src_ref=acc.at[p, s, to], dst_ref=col_in.at[p, where],
            send_sem=col_send.at[p, to], recv_sem=col_recv.at[p, where],
            device_id={"col": to}, device_id_type=MESH,
        )

    def pass_plane(q, b):
        @pl.when(b != j)
        def _():
            plane(q, b, slot).start()

    def start_own(q):
        x_copy(q).wait()

        @pl.when(r < R - 1)
        def _():
            up(q, r).start()

        @pl.when(r > 0)
        def _():
            down(q, r).start()

        pass_plane(q, r)

    for q in range(T):
        x_copy(q).start()
    for q in range(Q):
        k_copy(q).start()

    barrier = pltpu.get_barrier_semaphore()

    @pl.when(r < R - 1)
    def _():
        pl.semaphore_signal(barrier, inc=1, device_id={"row": r + 1}, device_id_type=MESH)

    @pl.when(r > 0)
    def _():
        pl.semaphore_signal(barrier, inc=1, device_id={"row": r - 1}, device_id_type=MESH)

    for other in range(C * S):
        @pl.when(other != j)
        def _():
            pl.semaphore_signal(
                barrier, inc=1,
                device_id={"col": other // S, "sub": other % S}, device_id_type=MESH,
            )

    ends = (r > 0).astype(jnp.int32) + (r < R - 1).astype(jnp.int32)
    pl.semaphore_wait(barrier, C * S - 1 + ends)

    def pass_on(q, t):
        below = r - t
        above = r + t

        @pl.when(below >= 0)
        def _():
            up(q, below).wait_recv()

            @pl.when(r < R - 1)
            def _():
                up(q, below).start()

            pass_plane(q, below)

        @pl.when(above < R)
        def _():
            down(q, above).wait_recv()

            @pl.when(r > 0)
            def _():
                down(q, above).start()

            pass_plane(q, above)

    def load_sources(q):
        for g in range(C * S):
            at = pl.ds(g * B, B)

            def put(value):
                high, low = split(value)
                xhigh[at, :] = high
                xlow[at, :] = low

            @pl.when(g != slot)
            def _():
                plane(q, j, g).wait_recv()
                put(wide[q, g])

            @pl.when(g == slot)
            def _():
                put(held[q, j])

    def tile(q, p):
        khigh, klow = split(kern[q % Q, targets(p), :])
        high = xhigh[...]
        part = times(high, khigh) + (times(high, klow) + times(xlow[...], khigh))
        at = (q // Q) * N + p
        acc[at] = acc[at] + part.reshape(S, C, B, NW)

    def add_pair(p):
        pair(p).wait_recv()
        acc[p, s] = acc[p, s] + pair_in[p]
        for to in range(C):
            @pl.when(to != c)
            def _():
                across(p, to, c).start()

    start_own(0)
    if T > 1:
        start_own(1)

    def clear(p, carry):
        acc[p] = jnp.zeros_like(acc[p])
        return carry

    lax.fori_loop(0, H * N, clear, 0)
    cuts = [(N * t) // (R - 1) for t in range(R)]

    def chunk(q, carry):
        done = (q - 1) // Q

        for t in range(1, R):
            pass_on(q, t)
            if t == 1:
                @pl.when(q + 2 < T)
                def _():
                    start_own(q + 2)

                @pl.when(q > 0)
                def _():
                    load_sources(q - 1)

                @pl.when((q > 0) & (q <= Q))
                def _():
                    k_copy(q - 1).wait()

            if cuts[t] > cuts[t - 1]:
                @pl.when(q > 0)
                def _():
                    def run(p, inner):
                        tile(q - 1, p)

                        @pl.when(q % Q == 0)
                        def _():
                            pair(done * N + p).start()

                        return inner

                    lax.fori_loop(cuts[t - 1], cuts[t], run, 0)

                @pl.when((q > Q) & (q % Q == 1 % Q))
                def _():
                    def run(p, inner):
                        add_pair((done - 1) * N + p)
                        return inner

                    lax.fori_loop(cuts[t - 1], cuts[t], run, 0)
        return carry

    lax.fori_loop(0, T, chunk, 0)
    load_sources(T - 1)
    if H == 1:
        k_copy(Q - 1).wait()

    def last(p, carry):
        tile(T - 1, p)
        pair((H - 1) * N + p).start()

        @pl.when(p > 0)
        def _():
            add_pair((H - 1) * N + p - 1)

        return carry

    lax.fori_loop(0, N, last, 0)
    add_pair(H * N - 1)

    def finish(p, carry):
        at = (part_of((p // N) * Q), targets(p % N))
        total = acc[p, s, c]
        out_ref[at] = total
        for other in range(C):
            @pl.when(other != c)
            def _():
                across(p, c, other).wait_recv()
                out_ref[at] = out_ref[at] + col_in[p, other]
        return carry

    lax.fori_loop(0, H * N, finish, 0)

    def drain_sums(p, carry):
        pair(p).wait_send()
        for to in range(C):
            @pl.when(to != c)
            def _():
                across(p, to, c).wait_send()
        return carry

    lax.fori_loop(0, H * N, drain_sums, 0)

    def drain(q, carry):
        for b in range(R):
            @pl.when((b <= r) & (r < R - 1))
            def _():
                up(q, b).wait_send()

            @pl.when((b >= r) & (r > 0))
            def _():
                down(q, b).wait_send()

            @pl.when(b != j)
            def _():
                plane(q, b, slot).wait_send()
        return carry

    lax.fori_loop(0, T, drain, 0)


def cut_of(D, most):
    lanes = D // 128
    for count in range(most, 1, -1):
        if D % 128 == 0 and lanes % count == 0:
            return count
    return 1


def step_call(R, C, S, rates, kernel):
    B, D = rates.shape
    H = 1
    B = B // H
    Q, N = cut_of(D, 6), cut_of(D, 6)
    assert Q > 1
    T, CW, NW = H * Q, D // Q, D // N
    dma = pltpu.SemaphoreType.DMA
    f32, b16 = jnp.float32, jnp.bfloat16
    return pl.pallas_call(
        functools.partial(step_kernel, R, C, S, H, Q, N),
        out_shape=jax.ShapeDtypeStruct(rates.shape, f32),
        in_specs=[pl.BlockSpec(memory_space=pl.ANY)] * 2,
        out_specs=pl.BlockSpec(memory_space=pltpu.VMEM),
        scratch_shapes=[
            pltpu.VMEM((T, R, B, CW), f32),
            pltpu.VMEM((T, C * S, B, CW), f32),
            pltpu.VMEM((Q, D, CW), f32),
            pltpu.VMEM((C * S * B, CW), b16),
            pltpu.VMEM((C * S * B, CW), b16),
            pltpu.VMEM((H * N, S, C, B, NW), f32),
            pltpu.VMEM((H * N, C, B, NW), f32),
            pltpu.VMEM((H * N, C, B, NW), f32),
            dma((T,)),
            dma((Q,)),
            dma((T, R)),
            dma((T, R)),
            dma((T, R)),
            dma((T, C * S)),
            dma((T, R)),
            dma((H * N,)),
            dma((H * N,)),
            dma((H * N, C)),
            dma((H * N, C)),
        ],
        compiler_params=pltpu.CompilerParams(
            collective_id=0, has_side_effects=True, vmem_limit_bytes=62 * 1024 * 1024
        ),
    )(rates, kernel)


def per_device(R, C, S, kernel, log_rate, state, base_stress, friction, region, adjacency):
    rows = kernel.shape[0]
    partner = adjacency - lax.axis_index("row") * rows
    volume = (region == 1)[None, :]
    fric = friction[None, :]

    first = step_call(R, C, S, jnp.exp(log_rate), kernel)
    section_one = solve(
        log_rate, state, coupled(base_stress, step_size, (first,), partner), fric, volume
    )
    second = step_call(R, C, S, jnp.exp(section_one), kernel)
    stress = coupled(base_stress, 0.5 * step_size, (first, second), partner)
    final_rate = solve(section_one, state, stress, fric, volume)
    return (final_rate, stress)


def solution(mesh):
    R, C, S = mesh.shape["row"], mesh.shape["col"], mesh.shape["sub"]
    assert R == C * S and S == 2
    in_specs = (
        P("row", ("col", "sub")),
        P(("member", "col", "sub"), "row"),
        P(("member", "col", "sub"), "row"),
        P(("member", "col", "sub"), "row"),
        P("row"),
        P("row"),
        P("row"),
    )
    out_specs = (P(("member", "col", "sub"), "row"), P(("member", "col", "sub"), "row"))
    return jax.shard_map(
        functools.partial(per_device, R, C, S),
        mesh=mesh, in_specs=in_specs, out_specs=out_specs, check_vma=False,
    )
```
